32 devices in a mesh: pipe: 2 (over y), ctx: 16 (over z, x, core).
Axes of the slice: x: 2, y: 2, z: 4, core: 2. Of those that a mesh axis runs over, the one named last changes fastest.
Arguments:
- saved_qkv: bfloat16 [2, 3, 2048, 2048], P('pipe', None, 'ctx'), may hold values from -6 to 6
- handed: bfloat16 [2, 2048, 2048], P('pipe', 'ctx'), may hold values from -6 to 6
- long_filter: bfloat16 [2, 128, 128], P('pipe'), may hold values from -0.5 to 0.5
- short_filter: bfloat16 [2, 3, 3, 2048], P('pipe'), may hold values from -3.5 to 3.5
- doc_lengths: int32 [16], replicated, may hold values from 1 to 512, 2048 in all
Outputs:
- grad_pre: bfloat16 [2, 3, 2048, 2048], P('pipe', None, 'ctx')
- filter_grad: float32 [2, 128, 128], P('pipe')
The draws below stay inside these ranges and needn't reach their ends.
Inputs may be any that keep to these rules, and one draw needn't show every extreme that they name: `doc_lengths`: documents lie end to end and sum to 2048 tokens; the longest has exactly 512 tokens.
All inputs are finite; a program needn't handle non-finite values.
Results may differ from the reference program's by a relative error of at most 0.0058.
Values may be sent and summed in bfloat16 or wider, within the bound.
A program may use at most 64 MiB of HBM per device.

```python
import math
import jax
import jax.numpy as jnp
import numpy as np
from jax import lax

C = 2048
GCH = 16
TAPS = 128
SHORT = 3
L_DEV = 128
GROUPS = 128
SEQ = 2048
SECTIONS = 2
NDOCS = 16


def block_levels(stream_key, shape, shards, least, top_value):
    level = 1.0
    for axis_at, shards_of in shards:
        draws = jax.random.uniform(jax.random.fold_in(jax.random.fold_in(stream_key, 6), axis_at), (shards_of,), jnp.float32, least / len(shards), top_value / len(shards))
        level = level * jnp.repeat(jnp.exp(draws), shape[axis_at] // shards_of).reshape((-1,) + (1,) * (len(shape) - 1 - axis_at))
    return level


def split_up(count, total, limit, lean):
    portions = [(1 << 20) // math.isqrt(rank ** lean) + 1 for rank in range(2, count + 1)]
    spare, counts = total - limit - (count - 1), [1] * (count - 1)
    while spare > 0:
        movable = [i for i in range(count - 1) if counts[i] < limit]
        pool, left = sum([portions[i] for i in movable]), spare
        for i in movable:
            addition = min(limit - counts[i], max(1, left * portions[i] // pool), spare)
            counts[i] = counts[i] + addition
            spare = spare - addition
    return np.array([limit] + counts)


def ragged(stream_key, count, total, reach, lean):
    if count == 2:
        one = jax.random.randint(stream_key, (), max(1, total - reach), min(reach, total - 1) + 1)
        return jnp.stack([one, total - one])
    tallies = jnp.asarray(split_up(count, total, reach, lean), jnp.int32)
    twos = (count - 1) // 2
    source_of, taker = tallies[1:1 + 2 * twos:2], tallies[2:2 + 2 * twos:2]
    margin = jnp.minimum(source_of - 1, reach - taker)
    moved = jax.random.randint(jax.random.fold_in(stream_key, 1), (twos,), 0, 1 << 20) % (margin + 1)
    tallies = tallies.at[1:1 + 2 * twos:2].set(source_of - moved).at[2:2 + 2 * twos:2].set(taker + moved)
    return tallies[jax.random.permutation(jax.random.fold_in(stream_key, 2), count)]


def bell_draw(own_key, extent, spread, reach, cuts=(), kind=jnp.bfloat16):
    loudness = block_levels(own_key, extent, cuts, -0.22, 0.18) if cuts else 1.0
    result = jax.random.normal(own_key, extent, jnp.float32) * spread * loudness
    return jnp.minimum(jnp.maximum(result, -reach), reach).astype(kind)


def setup_inputs(seed: int = 0) -> dict:
    streams_of = jax.random.split(jax.random.key(seed), 6)
    return {
        "saved_qkv": bell_draw(streams_of[0], (SECTIONS, 3, SEQ, C), 1.0, 6.0, ((0, 2), (2, 16))),
        "handed": bell_draw(streams_of[1], (SECTIONS, SEQ, C), 1.0, 6.0, ((0, 2), (1, 16))),
        "long_filter": bell_draw(streams_of[2], (SECTIONS, TAPS, GROUPS), TAPS ** -0.5, 0.5, ((0, 2),)),
        "short_filter": bell_draw(streams_of[3], (SECTIONS, 3, SHORT, C), SHORT ** -0.5, 3.5, ((0, 2),)),
        "doc_lengths": ragged(streams_of[4], NDOCS, SEQ, 4 * L_DEV, 2).astype(jnp.int32),
    }


def doc_positions(doc_lengths):
    starts = (jnp.cumsum(doc_lengths) - doc_lengths).astype(jnp.int32)
    global_rows = jnp.arange(SEQ, dtype=jnp.int32)
    latest = lax.optimization_barrier(jnp.max(jnp.where(starts[None, :] <= global_rows[:, None], starts[None, :], 0), axis=1))
    return (global_rows - latest).astype(jnp.int32)

def one_section(position, section_args):
    saved_rows, incoming, filt, short_taps = section_args
    query_rows = saved_rows[0].astype(jnp.float32)
    key_rows = saved_rows[1].astype(jnp.float32)
    value_rows = saved_rows[2].astype(jnp.float32)
    product = (key_rows * value_rows).astype(jnp.bfloat16).astype(jnp.float32)
    filt_wide = filt.astype(jnp.float32)
    padded_product = jnp.concatenate([jnp.zeros((TAPS, C), jnp.float32), product], axis=0)
    tap_index = jnp.arange(TAPS, dtype=jnp.int32)

    def forward_step(total, lag):
        shifted = lax.dynamic_slice_in_dim(padded_product, (TAPS - lag).astype(jnp.int32), SEQ, 0)
        weights = jnp.repeat(filt_wide[lag], GCH)
        usable = (lag <= position)[:, None]
        return (total + jnp.where(usable, shifted * weights[None, :], 0.0), None)
    conv_out, _ = lax.scan(forward_step, jnp.zeros((SEQ, C), jnp.float32), tap_index)
    incoming_wide = incoming.astype(jnp.float32)
    conv_grad = (incoming_wide * query_rows).astype(jnp.bfloat16).astype(jnp.float32)
    query_grad = (incoming_wide * conv_out).astype(jnp.bfloat16)
    padded_grad = jnp.concatenate([conv_grad, jnp.zeros((TAPS, C), jnp.float32)], axis=0)
    padded_pos = jnp.concatenate([position, jnp.full((TAPS,), -1, jnp.int32)])

    def backward_step(total, lag):
        ahead = lax.dynamic_slice_in_dim(padded_grad, lag, SEQ, 0)
        ahead_pos = lax.dynamic_slice_in_dim(padded_pos, lag, SEQ, 0)
        weights = jnp.repeat(filt_wide[lag], GCH)
        total = total + jnp.where((lag <= ahead_pos)[:, None], ahead * weights[None, :], 0.0)
        behind = lax.dynamic_slice_in_dim(padded_product, (TAPS - lag).astype(jnp.int32), SEQ, 0)
        pair = lax.optimization_barrier(jnp.sum((conv_grad * behind).reshape(SEQ, GROUPS, GCH), axis=2)).astype(jnp.bfloat16)
        pair = lax.optimization_barrier(pair).astype(jnp.float32)
        column = lax.optimization_barrier(jnp.sum(jnp.where((lag <= position)[:, None], pair, 0.0), axis=0))
        return (total, column)
    mixed_grad, filter_terms = lax.scan(backward_step, jnp.zeros((SEQ, C), jnp.float32), tap_index)
    key_grad = (mixed_grad * value_rows).astype(jnp.bfloat16)
    value_grad = (mixed_grad * key_rows).astype(jnp.bfloat16)
    stacked = jnp.stack([query_grad, key_grad, value_grad]).astype(jnp.float32)
    padded_stack = jnp.concatenate([stacked, jnp.zeros((3, SHORT - 1, C), jnp.float32)], axis=1)
    short_pos = jnp.concatenate([position, jnp.full((SHORT - 1,), -1, jnp.int32)])
    total = jnp.zeros((3, SEQ, C), jnp.float32)
    for shift_by in range(SHORT):
        usable = (shift_by <= short_pos[shift_by:shift_by + SEQ])[None, :, None]
        weights = short_taps[:, shift_by].astype(jnp.float32)[:, None, :]
        total = total + jnp.where(usable, weights * padded_stack[:, shift_by:shift_by + SEQ], 0.0)
    return (total.astype(jnp.bfloat16), filter_terms / math.sqrt(SEQ * GCH))

def reference(saved_qkv, handed, long_filter, short_filter, doc_lengths):
    position = doc_positions(doc_lengths)
    incoming_all = jnp.roll(handed, -1, axis=0)
    grad_pre, filter_grad = lax.map(lambda section_args: one_section(position, section_args), (saved_qkv, incoming_all, long_filter, short_filter))
    return (grad_pre, filter_grad)
```

```python
import functools
import math

import jax
import jax.numpy as jnp
from jax import lax
from jax.experimental import pallas as pl
from jax.experimental.pallas import tpu as pltpu
from jax.sharding import PartitionSpec as P

MESH = pl.DeviceIdType.MESH
F32 = jnp.float32
BF16 = jnp.bfloat16
LANES = 128
RIM = 8


def positions(rows, docs_ref):
    latest = jnp.zeros(rows.shape, jnp.int32)
    start = jnp.int32(0)
    for doc in range(docs_ref.shape[0]):
        latest = jnp.maximum(latest, jnp.where(start <= rows, start, 0))
        start = start + docs_ref[doc]
    return rows - latest


def kernel(
    sections, devices, chunks,
    docs_ref, qkv_hbm, handed_hbm, filt_ref, short_ref,
    out_hbm, fg_ref,
    qkv, inc, zz, gg, ysc, dsc, obuf, lhs, lhs3, fdir, frev, shortf,
    m_own, m_prev, t_own, t_next, r_own, r_prev, u_rows,
    acc, part, parts_in, gath,
    in_sem, out_sem, inc_s, inc_r, z_s, z_r, g_s, g_r, rim_s, rim_r, rs_s, rs_r, ag_s, ag_r,
):
    sec = lax.axis_index("pipe")
    me = lax.axis_index("ctx")
    count, channels = inc.shape
    groups = fdir.shape[0]
    members = channels // groups
    per_tile = LANES // members
    wide = channels // chunks
    tiles = wide // LANES
    share = groups // devices
    first, last = me == 0, me == devices - 1
    ahead = lax.rem(sec + sections - 1, sections)
    behind = lax.rem(sec + 1, sections)

    loads = [
        pltpu.make_async_copy(qkv_hbm.at[0, i], qkv.at[i], in_sem.at[i]) for i in range(3)
    ]
    for i in (1, 2, 0):
        loads[i].start()

    barrier = pltpu.get_barrier_semaphore()
    pl.semaphore_signal(barrier, inc=1, device_id={"pipe": behind}, device_id_type=MESH)

    def greet(k, carry):
        peer = lax.rem(me + k, devices)
        pl.semaphore_signal(barrier, inc=1, device_id={"ctx": peer}, device_id_type=MESH)
        return carry

    lax.fori_loop(1, devices, greet, 0)
    pl.semaphore_wait(barrier, devices)

    def cols(c):
        return pl.ds(c * wide, wide)

    def send_inc(c):
        return pltpu.make_async_remote_copy(
            handed_hbm.at[0, :, cols(c)], inc.at[:, cols(c)], inc_s.at[c], inc_r.at[c],
            device_id={"pipe": ahead}, device_id_type=MESH)

    def send_z(c):
        return pltpu.make_async_remote_copy(
            zz.at[pl.ds(0, count), cols(c)], zz.at[pl.ds(count, count), cols(c)],
            z_s.at[c], z_r.at[c],
            device_id={"ctx": lax.rem(me + 1, devices)}, device_id_type=MESH)

    def send_g(c):
        return pltpu.make_async_remote_copy(
            gg.at[pl.ds(0, count), cols(c)], gg.at[pl.ds(count, count), cols(c)],
            g_s.at[c], g_r.at[c],
            device_id={"ctx": lax.rem(me + devices - 1, devices)}, device_id_type=MESH)

    def send_rim(c):
        return pltpu.make_async_remote_copy(
            dsc.at[:, pl.ds(0, RIM), cols(c)], dsc.at[:, pl.ds(count, RIM), cols(c)],
            rim_s.at[c], rim_r.at[c],
            device_id={"ctx": lax.rem(me + devices - 1, devices)}, device_id_type=MESH)

    def send_part(k):
        peer = lax.rem(me + k, devices)
        return pltpu.make_async_remote_copy(
            part.at[peer], parts_in.at[k], rs_s.at[k], rs_r.at[k],
            device_id={"ctx": peer}, device_id_type=MESH)

    def send_sum(k):
        peer = lax.rem(me + k, devices)
        return pltpu.make_async_remote_copy(
            gath.at[me], gath.at[me], ag_s.at[k], ag_r.at[k],
            device_id={"ctx": peer}, device_id_type=MESH)

    def take_sum(k):
        peer = lax.rem(me + devices - k, devices)
        return pltpu.make_async_remote_copy(
            gath.at[peer], gath.at[peer], ag_s.at[k], ag_r.at[k],
            device_id={"ctx": lax.rem(me + k, devices)}, device_id_type=MESH)

    for c in range(chunks):
        send_inc(c).start()

    loads[1].wait()
    loads[2].wait()
    for c in range(chunks):
        z = qkv[1, :, cols(c)].astype(F32) * qkv[2, :, cols(c)].astype(F32)
        zz[pl.ds(0, count), cols(c)] = z.astype(BF16)

        @pl.when(jnp.logical_not(last))
        def _():
            send_z(c).start()

    @pl.when(first)
    def _():
        zz[pl.ds(count, count), :] = jnp.zeros((count, channels), BF16)

    @pl.when(last)
    def _():
        gg[pl.ds(count, count), :] = jnp.zeros((count, channels), BF16)
        dsc[:, pl.ds(count, RIM), :] = jnp.zeros((3, RIM, channels), F32)

    square = (count, count)
    down = lax.broadcasted_iota(jnp.int32, square, 0)
    across = lax.broadcasted_iota(jnp.int32, square, 1)
    base = me * count

    def one(flag):
        return jnp.where(flag, 1.0, 0.0).astype(F32)

    pos_down = positions(base + down, docs_ref)
    lag = down - across
    m_own[...] = one((lag >= 0) & (lag <= pos_down)).astype(BF16)
    m_prev[...] = one((lag < 0) & (lag + count <= pos_down)).astype(BF16)
    turned = count - 1 - down
    pos_turned = positions(base + turned, docs_ref)
    lag = turned - across
    r_own[...] = one((lag >= 0) & (lag <= pos_turned))
    r_prev[...] = one((lag < 0) & (lag + count <= pos_turned))
    line = lax.broadcasted_iota(jnp.int32, (8, count), 1)
    pos_line = positions(base + line, docs_ref)[0:1]
    pos_ahead = positions(base + count + line, docs_ref)[0:1]
    lag = across - down
    t_own[...] = one((lag >= 0) & (lag <= pos_line)).astype(BF16)
    more = jnp.where(last, 0, 1)
    t_next[...] = one((lag < 0) & (lag + count <= pos_ahead) & (more > 0)).astype(BF16)
    for j in range(1, u_rows.shape[0] + 1):
        rows = base + down[:, :LANES] + j
        u_rows[j - 1] = one((j <= positions(rows, docs_ref)) & (rows < devices * count))
    straight = one(down == across).astype(BF16)
    lapped = one((down + across == 0) | (down + across == count)).astype(BF16)
    flip = one(down + across == count - 1)
    sides = (((0,), (0,)), ((), ()))
    filt = filt_ref[0]
    fdir[...] = lax.dot_general(filt, straight, sides, preferred_element_type=F32)
    frev[...] = lax.dot_general(filt, lapped, sides, preferred_element_type=F32)
    shortf[...] = short_ref[0].astype(F32)
    lane_group = lax.broadcasted_iota(jnp.int32, (count, LANES), 1) // members

    def toeplitz(source, tile, near, far):
        block = source[pl.ds(pl.multiple_of(tile * per_tile, per_tile), per_tile), :]
        for g in range(per_tile):
            full = jnp.broadcast_to(block[g:g + 1], square)
            ring = pltpu.roll(full, 0, 1, stride=1, stride_axis=0).astype(BF16)
            lhs[g * count:(g + 1) * count, :count] = ring * near[...]
            lhs[g * count:(g + 1) * count, count:] = ring * far[...]

    def picked(product):
        total = product[:count]
        for g in range(1, per_tile):
            total = jnp.where(lane_group == g, product[g * count:(g + 1) * count], total)
        return total

    def lanes(tile):
        return pl.ds(pl.multiple_of(tile * LANES, LANES), LANES)

    for c in range(chunks):
        @pl.when(jnp.logical_not(first))
        def _():
            send_z(c).wait_recv()

        def forward(i, carry):
            tile = c * tiles + i
            toeplitz(frev, tile, m_own, m_prev)
            product = jnp.dot(lhs[...], zz[:, lanes(tile)], preferred_element_type=F32)
            ysc[:, lanes(tile)] = picked(product)
            return carry

        lax.fori_loop(0, tiles, forward, 0)

    loads[0].wait()
    for c in range(chunks):
        send_inc(c).wait_recv()
        wide_inc = inc[:, cols(c)].astype(F32)
        gg[pl.ds(0, count), cols(c)] = (wide_inc * qkv[0, :, cols(c)].astype(F32)).astype(BF16)

        @pl.when(jnp.logical_not(first))
        def _():
            send_g(c).start()

        dsc[0, pl.ds(0, count), cols(c)] = (wide_inc * ysc[:, cols(c)]).astype(BF16).astype(F32)

        def pairs(i, carry):
            tile = c * tiles + i
            own = gg[pl.ds(0, count), lanes(tile)]
            back = jnp.dot(flip.astype(BF16), own, preferred_element_type=F32)
            for g in range(per_tile):
                lhs3[g * count:(g + 1) * count, :] = jnp.where(
                    lane_group == g, back, 0.0).astype(BF16)
            product = lax.dot_general(
                lhs3[...], zz[:, lanes(tile)], (((1,), (1,)), ((), ())),
                preferred_element_type=F32)
            sums = []
            for g in range(per_tile):
                near = product[g * count:(g + 1) * count, :count]
                far = product[g * count:(g + 1) * count, count:]
                both = near * r_own[...] + far * r_prev[...]
                slid = pltpu.roll(both, 0, 1, stride=1, stride_axis=0)
                sums.append(jnp.sum(slid, axis=0, keepdims=True))
            acc[pl.ds(pl.multiple_of(tile * per_tile, per_tile), per_tile), :] = (
                jnp.concatenate(sums, axis=0))
            return carry

        lax.fori_loop(0, tiles, pairs, 0)

    for d in range(devices):
        part[d] = acc[d * share:(d + 1) * share, :]

    def start_part(k, carry):
        send_part(k).start()
        return carry

    lax.fori_loop(1, devices, start_part, 0)

    for c in range(chunks):
        @pl.when(jnp.logical_not(last))
        def _():
            send_g(c).wait_recv()

        def backward(i, carry):
            tile = c * tiles + i
            toeplitz(fdir, tile, t_own, t_next)
            product = jnp.dot(lhs[...], gg[:, lanes(tile)], preferred_element_type=F32)
            mixed = picked(product)
            key = qkv[1, :, lanes(tile)].astype(F32)
            value = qkv[2, :, lanes(tile)].astype(F32)
            dsc[1, pl.ds(0, count), lanes(tile)] = (mixed * value).astype(BF16).astype(F32)
            dsc[2, pl.ds(0, count), lanes(tile)] = (mixed * key).astype(BF16).astype(F32)
            return carry

        lax.fori_loop(0, tiles, backward, 0)

        @pl.when(jnp.logical_not(first))
        def _():
            send_rim(c).start()

    def land_part(k, total):
        send_part(k).wait_recv()
        return total + parts_in[k]

    gath[me] = lax.fori_loop(1, devices, land_part, part[me])

    def start_sum(k, carry):
        send_sum(k).start()
        return carry

    lax.fori_loop(1, devices, start_sum, 0)

    def store(c):
        return pltpu.make_async_copy(
            obuf.at[:, :, cols(c)], out_hbm.at[0, :, :, cols(c)], out_sem.at[c])

    for c in range(chunks):
        @pl.when(jnp.logical_not(last))
        def _():
            send_rim(c).wait_recv()

        def short(i, carry):
            tile = c * tiles + i
            for s in range(3):
                total = dsc[s, pl.ds(0, count), lanes(tile)] * shortf[s, pl.ds(0, 1), lanes(tile)]
                for j in range(1, u_rows.shape[0] + 1):
                    moved = dsc[s, pl.ds(j, count), lanes(tile)]
                    weight = shortf[s, pl.ds(j, 1), lanes(tile)]
                    total = total + (moved * weight) * u_rows[j - 1]
                obuf[s, :, lanes(tile)] = total.astype(BF16)
            return carry

        lax.fori_loop(0, tiles, short, 0)
        store(c).start()

    def land_sum(k, carry):
        take_sum(k).wait_recv()
        return carry

    lax.fori_loop(1, devices, land_sum, 0)
    for d in range(devices):
        acc[d * share:(d + 1) * share, :] = gath[d]
    summed = lax.dot_general(
        flip, acc[...], (((1,), (1,)), ((), ())),
        preferred_element_type=F32, precision=lax.Precision.HIGHEST)
    fg_ref[0] = summed / math.sqrt(count * devices * members)

    def left(k, carry):
        send_part(k).wait_send()
        send_sum(k).wait_send()
        return carry

    lax.fori_loop(1, devices, left, 0)
    for c in range(chunks):
        send_inc(c).wait_send()
        store(c).wait()

        @pl.when(jnp.logical_not(last))
        def _():
            send_z(c).wait_send()

        @pl.when(jnp.logical_not(first))
        def _():
            send_g(c).wait_send()
            send_rim(c).wait_send()


def body(sections, devices, saved_qkv, handed, long_filter, short_filter, doc_lengths):
    _, _, count, channels = saved_qkv.shape
    _, taps, groups = long_filter.shape
    short_taps = short_filter.shape[2]
    assert taps == count and groups % devices == 0
    chunks = max(1, math.gcd(channels // LANES, 4))
    per_tile = LANES // (channels // groups)
    share = groups // devices
    dma = pltpu.SemaphoreType.DMA
    vmem = pltpu.VMEM
    hbm = pl.BlockSpec(memory_space=pl.ANY)
    local = pl.BlockSpec(memory_space=pltpu.VMEM)
    return pl.pallas_call(
        functools.partial(kernel, sections, devices, chunks),
        out_shape=(
            jax.ShapeDtypeStruct(saved_qkv.shape, BF16),
            jax.ShapeDtypeStruct(long_filter.shape, F32),
        ),
        in_specs=[pl.BlockSpec(memory_space=pltpu.SMEM), hbm, hbm, local, local],
        out_specs=(hbm, local),
        scratch_shapes=[
            vmem((3, count, channels), BF16),
            vmem((count, channels), BF16),
            vmem((2 * count, channels), BF16),
            vmem((2 * count, channels), BF16),
            vmem((count, channels), F32),
            vmem((3, count + RIM, channels), F32),
            vmem((3, count, channels), BF16),
            vmem((per_tile * count, 2 * count), BF16),
            vmem((per_tile * count, LANES), BF16),
            vmem((groups, count), F32),
            vmem((groups, count), F32),
            vmem((3, short_taps, channels), F32),
            vmem((count, count), BF16),
            vmem((count, count), BF16),
            vmem((count, count), BF16),
            vmem((count, count), BF16),
            vmem((count, count), F32),
            vmem((count, count), F32),
            vmem((short_taps - 1, count, LANES), F32),
            vmem((groups, count), F32),
            vmem((devices, share, count), F32),
            vmem((devices, share, count), F32),
            vmem((devices, share, count), F32),
            dma((3,)), dma((chunks,)),
            dma((chunks,)), dma((chunks,)),
            dma((chunks,)), dma((chunks,)),
            dma((chunks,)), dma((chunks,)),
            dma((chunks,)), dma((chunks,)),
            dma((devices,)), dma((devices,)),
            dma((devices,)), dma((devices,)),
        ],
        compiler_params=pltpu.CompilerParams(collective_id=0, has_side_effects=True),
    )(doc_lengths, saved_qkv, handed, long_filter, short_filter)


def solution(mesh):
    return jax.shard_map(
        functools.partial(body, mesh.shape["pipe"], mesh.shape["ctx"]),
        mesh=mesh,
        in_specs=(
            P("pipe", None, "ctx", None),
            P("pipe", "ctx", None),
            P("pipe", None, None),
            P("pipe", None, None, None),
            P(),
        ),
        out_specs=(P("pipe", None, "ctx", None), P("pipe", None, None)),
        check_vma=False,
    )
```

```python
import functools
import math

import jax
import jax.numpy as jnp
from jax import lax
from jax.experimental import pallas as pl
from jax.experimental.pallas import tpu as pltpu
from jax.sharding import PartitionSpec as P

MESH = pl.DeviceIdType.MESH
F32 = jnp.float32
BF16 = jnp.bfloat16
LANES = 128
RIM = 8


def positions(rows, docs_ref):
    latest = jnp.zeros(rows.shape, jnp.int32)
    start = jnp.int32(0)
    for doc in range(docs_ref.shape[0]):
        latest = jnp.maximum(latest, jnp.where(start <= rows, start, 0))
        start = start + docs_ref[doc]
    return rows - latest


def kernel(
    sections, devices, chunks,
    docs_ref, qkv_hbm, handed_hbm, filt_ref, short_ref,
    out_hbm, fg_ref,
    qkv, inc, zz, gg, ysc, dsc, obuf, lhs, lhs3, fdir, frev, shortf,
    m_own, m_prev, t_own, t_next, r_own, r_prev, u_rows,
    acc, part, parts_in, gath,
    in_sem, out_sem, inc_s, inc_r, z_s, z_r, g_s, g_r, rim_s, rim_r, rs_s, rs_r, ag_s, ag_r,
):
    sec = lax.axis_index("pipe")
    me = lax.axis_index("ctx")
    count, channels = inc.shape
    groups = fdir.shape[0]
    members = channels // groups
    per_tile = LANES // members
    wide = channels // chunks
    tiles = wide // LANES
    share = groups // devices
    first, last = me == 0, me == devices - 1
    ahead = lax.rem(sec + sections - 1, sections)
    behind = lax.rem(sec + 1, sections)

    loads = [
        pltpu.make_async_copy(qkv_hbm.at[0, i], qkv.at[i], in_sem.at[i]) for i in range(3)
    ]
    for i in (1, 2, 0):
        loads[i].start()

    barrier = pltpu.get_barrier_semaphore()
    pl.semaphore_signal(barrier, inc=1, device_id={"pipe": behind}, device_id_type=MESH)

    def greet(k, carry):
        peer = lax.rem(me + k, devices)
        pl.semaphore_signal(barrier, inc=1, device_id={"ctx": peer}, device_id_type=MESH)
        return carry

    lax.fori_loop(1, devices, greet, 0)
    pl.semaphore_wait(barrier, devices)

    def cols(c):
        return pl.ds(c * wide, wide)

    def send_inc(c):
        return pltpu.make_async_remote_copy(
            handed_hbm.at[0, :, cols(c)], inc.at[:, cols(c)], inc_s.at[c], inc_r.at[c],
            device_id={"pipe": ahead}, device_id_type=MESH)

    def send_z(c):
        return pltpu.make_async_remote_copy(
            zz.at[pl.ds(0, count), cols(c)], zz.at[pl.ds(count, count), cols(c)],
            z_s.at[c], z_r.at[c],
            device_id={"ctx": lax.rem(me + 1, devices)}, device_id_type=MESH)

    def send_g(c):
        return pltpu.make_async_remote_copy(
            gg.at[pl.ds(0, count), cols(c)], gg.at[pl.ds(count, count), cols(c)],
            g_s.at[c], g_r.at[c],
            device_id={"ctx": lax.rem(me + devices - 1, devices)}, device_id_type=MESH)

    def send_rim(c):
        return pltpu.make_async_remote_copy(
            dsc.at[:, pl.ds(0, RIM), cols(c)], dsc.at[:, pl.ds(count, RIM), cols(c)],
            rim_s.at[c], rim_r.at[c],
            device_id={"ctx": lax.rem(me + devices - 1, devices)}, device_id_type=MESH)

    def send_part(k):
        peer = lax.rem(me + k, devices)
        return pltpu.make_async_remote_copy(
            part.at[peer], parts_in.at[k], rs_s.at[k], rs_r.at[k],
            device_id={"ctx": peer}, device_id_type=MESH)

    def send_sum(k):
        peer = lax.rem(me + k, devices)
        return pltpu.make_async_remote_copy(
            gath.at[me], gath.at[me], ag_s.at[k], ag_r.at[k],
            device_id={"ctx": peer}, device_id_type=MESH)

    def take_sum(k):
        peer = lax.rem(me + devices - k, devices)
        return pltpu.make_async_remote_copy(
            gath.at[peer], gath.at[peer], ag_s.at[k], ag_r.at[k],
            device_id={"ctx": lax.rem(me + k, devices)}, device_id_type=MESH)

    for c in range(chunks):
        send_inc(c).start()

    loads[1].wait()
    loads[2].wait()
    for c in range(chunks):
        z = qkv[1, :, cols(c)].astype(F32) * qkv[2, :, cols(c)].astype(F32)
        zz[pl.ds(0, count), cols(c)] = z.astype(BF16)

        @pl.when(jnp.logical_not(last))
        def _():
            send_z(c).start()

    @pl.when(first)
    def _():
        zz[pl.ds(count, count), :] = jnp.zeros((count, channels), BF16)

    @pl.when(last)
    def _():
        gg[pl.ds(count, count), :] = jnp.zeros((count, channels), BF16)
        dsc[:, pl.ds(count, RIM), :] = jnp.zeros((3, RIM, channels), F32)

    square = (count, count)
    down = lax.broadcasted_iota(jnp.int32, square, 0)
    across = lax.broadcasted_iota(jnp.int32, square, 1)
    base = me * count

    def one(flag):
        return jnp.where(flag, 1.0, 0.0).astype(F32)

    pos_down = positions(base + down, docs_ref)
    lag = down - across
    m_own[...] = one((lag >= 0) & (lag <= pos_down)).astype(BF16)
    m_prev[...] = one((lag < 0) & (lag + count <= pos_down)).astype(BF16)
    turned = count - 1 - down
    pos_turned = positions(base + turned, docs_ref)
    lag = turned - across
    r_own[...] = one((lag >= 0) & (lag <= pos_turned))
    r_prev[...] = one((lag < 0) & (lag + count <= pos_turned))
    line = lax.broadcasted_iota(jnp.int32, (8, count), 1)
    pos_line = positions(base + line, docs_ref)[0:1]
    pos_ahead = positions(base + count + line, docs_ref)[0:1]
    lag = across - down
    t_own[...] = one((lag >= 0) & (lag <= pos_line)).astype(BF16)
    more = jnp.where(last, 0, 1)
    t_next[...] = one((lag < 0) & (lag + count <= pos_ahead) & (more > 0)).astype(BF16)
    for j in range(1, u_rows.shape[0] + 1):
        rows = base + down[:, :LANES] + j
        u_rows[j - 1] = one((j <= positions(rows, docs_ref)) & (rows < devices * count))
    straight = one(down == across).astype(BF16)
    lapped = one((down + across == 0) | (down + across == count)).astype(BF16)
    flip = one(down + across == count - 1)
    sides = (((0,), (0,)), ((), ()))
    filt = filt_ref[0]
    fdir[...] = lax.dot_general(filt, straight, sides, preferred_element_type=F32)
    frev[...] = lax.dot_general(filt, lapped, sides, preferred_element_type=F32)
    shortf[...] = short_ref[0].astype(F32)
    lane_group = lax.broadcasted_iota(jnp.int32, (count, LANES), 1) // members

    def toeplitz(source, tile, near, far):
        block = source[pl.ds(pl.multiple_of(tile * per_tile, per_tile), per_tile), :]
        for g in range(per_tile):
            full = jnp.broadcast_to(block[g:g + 1], square)
            ring = pltpu.roll(full, 0, 1, stride=1, stride_axis=0).astype(BF16)
            lhs[g * count:(g + 1) * count, :count] = ring * near[...]
            lhs[g * count:(g + 1) * count, count:] = ring * far[...]

    def picked(product):
        total = product[:count]
        for g in range(1, per_tile):
            total = jnp.where(lane_group == g, product[g * count:(g + 1) * count], total)
        return total

    def lanes(tile):
        return pl.ds(pl.multiple_of(tile * LANES, LANES), LANES)

    for c in range(chunks):
        @pl.when(jnp.logical_not(first))
        def _():
            send_z(c).wait_recv()

        def forward(i, carry):
            tile = c * tiles + i
            toeplitz(frev, tile, m_own, m_prev)
            product = jnp.dot(lhs[...], zz[:, lanes(tile)], preferred_element_type=F32)
            ysc[:, lanes(tile)] = picked(product)
            return carry

        lax.fori_loop(0, tiles, forward, 0)

    def backward_chunk(c):
        @pl.when(jnp.logical_not(last))
        def _():
            send_g(c).wait_recv()

        def backward(i, carry):
            tile = c * tiles + i
            toeplitz(fdir, tile, t_own, t_next)
            product = jnp.dot(lhs[...], gg[:, lanes(tile)], preferred_element_type=F32)
            mixed = picked(product)
            key = qkv[1, :, lanes(tile)].astype(F32)
            value = qkv[2, :, lanes(tile)].astype(F32)
            dsc[1, pl.ds(0, count), lanes(tile)] = (mixed * value).astype(BF16).astype(F32)
            dsc[2, pl.ds(0, count), lanes(tile)] = (mixed * key).astype(BF16).astype(F32)
            return carry

        lax.fori_loop(0, tiles, backward, 0)

        @pl.when(jnp.logical_not(first))
        def _():
            send_rim(c).start()

    def store(c):
        return pltpu.make_async_copy(
            obuf.at[:, :, cols(c)], out_hbm.at[0, :, :, cols(c)], out_sem.at[c])

    def short_chunk(c):
        @pl.when(jnp.logical_not(last))
        def _():
            send_rim(c).wait_recv()

        def short(i, carry):
            tile = c * tiles + i
            for s in range(3):
                total = dsc[s, pl.ds(0, count), lanes(tile)] * shortf[s, pl.ds(0, 1), lanes(tile)]
                for j in range(1, u_rows.shape[0] + 1):
                    moved = dsc[s, pl.ds(j, count), lanes(tile)]
                    weight = shortf[s, pl.ds(j, 1), lanes(tile)]
                    total = total + (moved * weight) * u_rows[j - 1]
                obuf[s, :, lanes(tile)] = total.astype(BF16)
            return carry

        lax.fori_loop(0, tiles, short, 0)
        store(c).start()

    loads[0].wait()
    for c in range(chunks):
        send_inc(c).wait_recv()
        wide_inc = inc[:, cols(c)].astype(F32)
        gg[pl.ds(0, count), cols(c)] = (wide_inc * qkv[0, :, cols(c)].astype(F32)).astype(BF16)

        @pl.when(jnp.logical_not(first))
        def _():
            send_g(c).start()

        dsc[0, pl.ds(0, count), cols(c)] = (wide_inc * ysc[:, cols(c)]).astype(BF16).astype(F32)

        def pairs(i, carry):
            tile = c * tiles + i
            own = gg[pl.ds(0, count), lanes(tile)]
            back = jnp.dot(flip.astype(BF16), own, preferred_element_type=F32)
            for g in range(per_tile):
                lhs3[g * count:(g + 1) * count, :] = jnp.where(
                    lane_group == g, back, 0.0).astype(BF16)
            product = lax.dot_general(
                lhs3[...], zz[:, lanes(tile)], (((1,), (1,)), ((), ())),
                preferred_element_type=F32)
            sums = []
            for g in range(per_tile):
                near = product[g * count:(g + 1) * count, :count]
                far = product[g * count:(g + 1) * count, count:]
                both = near * r_own[...] + far * r_prev[...]
                slid = pltpu.roll(both, 0, 1, stride=1, stride_axis=0)
                sums.append(jnp.sum(slid, axis=0, keepdims=True))
            acc[pl.ds(pl.multiple_of(tile * per_tile, per_tile), per_tile), :] = (
                jnp.concatenate(sums, axis=0))
            return carry

        lax.fori_loop(0, tiles, pairs, 0)
        if c >= 2:
            backward_chunk(c - 2)

    for d in range(devices):
        part[d] = acc[d * share:(d + 1) * share, :]

    def start_part(k, carry):
        send_part(k).start()
        return carry

    lax.fori_loop(1, devices, start_part, 0)

    for c in range(max(chunks - 2, 0), chunks):
        backward_chunk(c)
    held = max(chunks - 2, 0)
    for c in range(held):
        short_chunk(c)

    def land_part(k, total):
        send_part(k).wait_recv()
        return total + parts_in[k]

    gath[me] = lax.fori_loop(1, devices, land_part, part[me])

    def start_sum(k, carry):
        send_sum(k).start()
        return carry

    lax.fori_loop(1, devices, start_sum, 0)

    for c in range(held, chunks):
        short_chunk(c)

    def land_sum(k, carry):
        take_sum(k).wait_recv()
        return carry

    lax.fori_loop(1, devices, land_sum, 0)
    for d in range(devices):
        acc[d * share:(d + 1) * share, :] = gath[d]
    summed = lax.dot_general(
        flip, acc[...], (((1,), (1,)), ((), ())),
        preferred_element_type=F32, precision=lax.Precision.HIGHEST)
    fg_ref[0] = summed / math.sqrt(count * devices * members)

    def left(k, carry):
        send_part(k).wait_send()
        send_sum(k).wait_send()
        return carry

    lax.fori_loop(1, devices, left, 0)
    for c in range(chunks):
        send_inc(c).wait_send()
        store(c).wait()

        @pl.when(jnp.logical_not(last))
        def _():
            send_z(c).wait_send()

        @pl.when(jnp.logical_not(first))
        def _():
            send_g(c).wait_send()
            send_rim(c).wait_send()


def body(sections, devices, saved_qkv, handed, long_filter, short_filter, doc_lengths):
    _, _, count, channels = saved_qkv.shape
    _, taps, groups = long_filter.shape
    short_taps = short_filter.shape[2]
    assert taps == count and groups % devices == 0
    chunks = max(1, math.gcd(channels // LANES, 8))
    per_tile = LANES // (channels // groups)
    share = groups // devices
    dma = pltpu.SemaphoreType.DMA
    vmem = pltpu.VMEM
    hbm = pl.BlockSpec(memory_space=pl.ANY)
    local = pl.BlockSpec(memory_space=pltpu.VMEM)
    return pl.pallas_call(
        functools.partial(kernel, sections, devices, chunks),
        out_shape=(
            jax.ShapeDtypeStruct(saved_qkv.shape, BF16),
            jax.ShapeDtypeStruct(long_filter.shape, F32),
        ),
        in_specs=[pl.BlockSpec(memory_space=pltpu.SMEM), hbm, hbm, local, local],
        out_specs=(hbm, local),
        scratch_shapes=[
            vmem((3, count, channels), BF16),
            vmem((count, channels), BF16),
            vmem((2 * count, channels), BF16),
            vmem((2 * count, channels), BF16),
            vmem((count, channels), F32),
            vmem((3, count + RIM, channels), F32),
            vmem((3, count, channels), BF16),
            vmem((per_tile * count, 2 * count), BF16),
            vmem((per_tile * count, LANES), BF16),
            vmem((groups, count), F32),
            vmem((groups, count), F32),
            vmem((3, short_taps, channels), F32),
            vmem((count, count), BF16),
            vmem((count, count), BF16),
            vmem((count, count), BF16),
            vmem((count, count), BF16),
            vmem((count, count), F32),
            vmem((count, count), F32),
            vmem((short_taps - 1, count, LANES), F32),
            vmem((groups, count), F32),
            vmem((devices, share, count), F32),
            vmem((devices, share, count), F32),
            vmem((devices, share, count), F32),
            dma((3,)), dma((chunks,)),
            dma((chunks,)), dma((chunks,)),
            dma((chunks,)), dma((chunks,)),
            dma((chunks,)), dma((chunks,)),
            dma((chunks,)), dma((chunks,)),
            dma((devices,)), dma((devices,)),
            dma((devices,)), dma((devices,)),
        ],
        compiler_params=pltpu.CompilerParams(collective_id=0, has_side_effects=True),
    )(doc_lengths, saved_qkv, handed, long_filter, short_filter)


def solution(mesh):
    return jax.shard_map(
        functools.partial(body, mesh.shape["pipe"], mesh.shape["ctx"]),
        mesh=mesh,
        in_specs=(
            P("pipe", None, "ctx", None),
            P("pipe", "ctx", None),
            P("pipe", None, None),
            P("pipe", None, None, None),
            P(),
        ),
        out_specs=(P("pipe", None, "ctx", None), P("pipe", None, None)),
        check_vma=False,
    )
```

```python
import functools
import math

import jax
import jax.numpy as jnp
from jax import lax
from jax.experimental import pallas as pl
from jax.experimental.pallas import tpu as pltpu
from jax.sharding import PartitionSpec as P

MESH = pl.DeviceIdType.MESH
F32 = jnp.float32
BF16 = jnp.bfloat16
LANES = 128
RIM = 8


def positions(rows, docs_ref):
    latest = jnp.zeros(rows.shape, jnp.int32)
    start = jnp.int32(0)
    for doc in range(docs_ref.shape[0]):
        latest = jnp.maximum(latest, jnp.where(start <= rows, start, 0))
        start = start + docs_ref[doc]
    return rows - latest


def kernel(
    sections, devices, chunks,
    docs_ref, qkv_hbm, handed_hbm, filt_ref, short_ref,
    out_hbm, fg_ref,
    qkv, inc, zz, gg, ysc, dsc, obuf, lhs, lhs3, fdir, frev, shortf,
    m_own, m_prev, t_own, t_next, r_own, r_prev, u_rows,
    acc, part, parts_in, gath,
    in_sem, out_sem, inc_s, inc_r, z_s, z_r, g_s, g_r, rim_s, rim_r, rs_s, rs_r, ag_s, ag_r, ready,
):
    sec = lax.axis_index("pipe")
    me = lax.axis_index("ctx")
    count, channels = inc.shape
    groups = fdir.shape[0]
    members = channels // groups
    per_tile = LANES // members
    wide = channels // chunks
    tiles = wide // LANES
    share = groups // devices
    first, last = me == 0, me == devices - 1
    ahead = lax.rem(sec + sections - 1, sections)
    behind = lax.rem(sec + 1, sections)

    loads = [
        pltpu.make_async_copy(qkv_hbm.at[0, i], qkv.at[i], in_sem.at[i]) for i in range(3)
    ]
    for i in (1, 2, 0):
        loads[i].start()

    barrier = pltpu.get_barrier_semaphore()
    pl.semaphore_signal(barrier, inc=1, device_id={"pipe": behind}, device_id_type=MESH)

    for step in (1, devices - 1):
        peer = lax.rem(me + step, devices)
        pl.semaphore_signal(barrier, inc=1, device_id={"ctx": peer}, device_id_type=MESH)
    pl.semaphore_wait(barrier, 3)

    reaches = []
    while 2 ** len(reaches) < devices // 2:
        reaches.append(2 ** len(reaches))

    def tell(r):
        if r < len(reaches):
            for step in (reaches[r], devices - reaches[r]):
                peer = lax.rem(me + step, devices)
                pl.semaphore_signal(
                    ready.at[r], inc=1, device_id={"ctx": peer}, device_id_type=MESH)

    def hear(r):
        if r < len(reaches):
            pl.semaphore_wait(ready.at[r], 2)

    def cols(c):
        return pl.ds(c * wide, wide)

    def send_inc(c):
        return pltpu.make_async_remote_copy(
            handed_hbm.at[0, :, cols(c)], inc.at[:, cols(c)], inc_s.at[c], inc_r.at[c],
            device_id={"pipe": ahead}, device_id_type=MESH)

    def send_z(c):
        return pltpu.make_async_remote_copy(
            zz.at[pl.ds(0, count), cols(c)], zz.at[pl.ds(count, count), cols(c)],
            z_s.at[c], z_r.at[c],
            device_id={"ctx": lax.rem(me + 1, devices)}, device_id_type=MESH)

    def send_g(c):
        return pltpu.make_async_remote_copy(
            gg.at[pl.ds(0, count), cols(c)], gg.at[pl.ds(count, count), cols(c)],
            g_s.at[c], g_r.at[c],
            device_id={"ctx": lax.rem(me + devices - 1, devices)}, device_id_type=MESH)

    def send_rim(c):
        return pltpu.make_async_remote_copy(
            dsc.at[:, pl.ds(0, RIM), cols(c)], dsc.at[:, pl.ds(count, RIM), cols(c)],
            rim_s.at[c], rim_r.at[c],
            device_id={"ctx": lax.rem(me + devices - 1, devices)}, device_id_type=MESH)

    def send_part(k):
        peer = lax.rem(me + k, devices)
        return pltpu.make_async_remote_copy(
            part.at[peer], parts_in.at[k], rs_s.at[k], rs_r.at[k],
            device_id={"ctx": peer}, device_id_type=MESH)

    def send_sum(k):
        peer = lax.rem(me + k, devices)
        return pltpu.make_async_remote_copy(
            gath.at[me], gath.at[me], ag_s.at[k], ag_r.at[k],
            device_id={"ctx": peer}, device_id_type=MESH)

    def take_sum(k):
        peer = lax.rem(me + devices - k, devices)
        return pltpu.make_async_remote_copy(
            gath.at[peer], gath.at[peer], ag_s.at[k], ag_r.at[k],
            device_id={"ctx": lax.rem(me + k, devices)}, device_id_type=MESH)

    for c in range(chunks):
        send_inc(c).start()
    tell(0)

    loads[1].wait()
    loads[2].wait()
    for c in range(chunks):
        z = qkv[1, :, cols(c)].astype(F32) * qkv[2, :, cols(c)].astype(F32)
        zz[pl.ds(0, count), cols(c)] = z.astype(BF16)

        @pl.when(jnp.logical_not(last))
        def _():
            send_z(c).start()

    @pl.when(first)
    def _():
        zz[pl.ds(count, count), :] = jnp.zeros((count, channels), BF16)

    @pl.when(last)
    def _():
        gg[pl.ds(count, count), :] = jnp.zeros((count, channels), BF16)
        dsc[:, pl.ds(count, RIM), :] = jnp.zeros((3, RIM, channels), F32)

    square = (count, count)
    down = lax.broadcasted_iota(jnp.int32, square, 0)
    across = lax.broadcasted_iota(jnp.int32, square, 1)
    base = me * count

    def one(flag):
        return jnp.where(flag, 1.0, 0.0).astype(F32)

    pos_down = positions(base + down, docs_ref)
    lag = down - across
    m_own[...] = one((lag >= 0) & (lag <= pos_down)).astype(BF16)
    m_prev[...] = one((lag < 0) & (lag + count <= pos_down)).astype(BF16)
    turned = count - 1 - down
    pos_turned = positions(base + turned, docs_ref)
    lag = turned - across
    r_own[...] = one((lag >= 0) & (lag <= pos_turned))
    r_prev[...] = one((lag < 0) & (lag + count <= pos_turned))
    line = lax.broadcasted_iota(jnp.int32, (8, count), 1)
    pos_line = positions(base + line, docs_ref)[0:1]
    pos_ahead = positions(base + count + line, docs_ref)[0:1]
    lag = across - down
    t_own[...] = one((lag >= 0) & (lag <= pos_line)).astype(BF16)
    more = jnp.where(last, 0, 1)
    t_next[...] = one((lag < 0) & (lag + count <= pos_ahead) & (more > 0)).astype(BF16)
    for j in range(1, u_rows.shape[0] + 1):
        rows = base + down[:, :LANES] + j
        u_rows[j - 1] = one((j <= positions(rows, docs_ref)) & (rows < devices * count))
    straight = one(down == across).astype(BF16)
    lapped = one((down + across == 0) | (down + across == count)).astype(BF16)
    flip = one(down + across == count - 1)
    sides = (((0,), (0,)), ((), ()))
    filt = filt_ref[0]
    fdir[...] = lax.dot_general(filt, straight, sides, preferred_element_type=F32)
    frev[...] = lax.dot_general(filt, lapped, sides, preferred_element_type=F32)
    shortf[...] = short_ref[0].astype(F32)
    lane_group = lax.broadcasted_iota(jnp.int32, (count, LANES), 1) // members

    def toeplitz(source, tile, near, far):
        block = source[pl.ds(pl.multiple_of(tile * per_tile, per_tile), per_tile), :]
        for g in range(per_tile):
            full = jnp.broadcast_to(block[g:g + 1], square)
            ring = pltpu.roll(full, 0, 1, stride=1, stride_axis=0).astype(BF16)
            lhs[g * count:(g + 1) * count, :count] = ring * near[...]
            lhs[g * count:(g + 1) * count, count:] = ring * far[...]

    def picked(product):
        total = product[:count]
        for g in range(1, per_tile):
            total = jnp.where(lane_group == g, product[g * count:(g + 1) * count], total)
        return total

    def lanes(tile):
        return pl.ds(pl.multiple_of(tile * LANES, LANES), LANES)

    for c in range(chunks):
        @pl.when(jnp.logical_not(first))
        def _():
            send_z(c).wait_recv()

        def forward(i, carry):
            tile = c * tiles + i
            toeplitz(frev, tile, m_own, m_prev)
            product = jnp.dot(lhs[...], zz[:, lanes(tile)], preferred_element_type=F32)
            ysc[:, lanes(tile)] = picked(product)
            return carry

        lax.fori_loop(0, tiles, forward, 0)
        hear(c)
        tell(c + 1)

    loads[0].wait()
    for c in range(chunks):
        send_inc(c).wait_recv()
        wide_inc = inc[:, cols(c)].astype(F32)
        gg[pl.ds(0, count), cols(c)] = (wide_inc * qkv[0, :, cols(c)].astype(F32)).astype(BF16)

        @pl.when(jnp.logical_not(first))
        def _():
            send_g(c).start()

        dsc[0, pl.ds(0, count), cols(c)] = (wide_inc * ysc[:, cols(c)]).astype(BF16).astype(F32)

        def pairs(i, carry):
            tile = c * tiles + i
            own = gg[pl.ds(0, count), lanes(tile)]
            back = jnp.dot(flip.astype(BF16), own, preferred_element_type=F32)
            for g in range(per_tile):
                lhs3[g * count:(g + 1) * count, :] = jnp.where(
                    lane_group == g, back, 0.0).astype(BF16)
            product = lax.dot_general(
                lhs3[...], zz[:, lanes(tile)], (((1,), (1,)), ((), ())),
                preferred_element_type=F32)
            sums = []
            for g in range(per_tile):
                near = product[g * count:(g + 1) * count, :count]
                far = product[g * count:(g + 1) * count, count:]
                both = near * r_own[...] + far * r_prev[...]
                slid = pltpu.roll(both, 0, 1, stride=1, stride_axis=0)
                sums.append(jnp.sum(slid, axis=0, keepdims=True))
            acc[pl.ds(pl.multiple_of(tile * per_tile, per_tile), per_tile), :] = (
                jnp.concatenate(sums, axis=0))
            return carry

        lax.fori_loop(0, tiles, pairs, 0)

    for r in range(chunks, len(reaches)):
        hear(r)
        tell(r + 1)
    for d in range(devices):
        part[d] = acc[d * share:(d + 1) * share, :]

    def start_part(k, carry):
        send_part(k).start()
        return carry

    lax.fori_loop(1, devices, start_part, 0)

    for c in range(chunks):
        @pl.when(jnp.logical_not(last))
        def _():
            send_g(c).wait_recv()

        def backward(i, carry):
            tile = c * tiles + i
            toeplitz(fdir, tile, t_own, t_next)
            product = jnp.dot(lhs[...], gg[:, lanes(tile)], preferred_element_type=F32)
            mixed = picked(product)
            key = qkv[1, :, lanes(tile)].astype(F32)
            value = qkv[2, :, lanes(tile)].astype(F32)
            dsc[1, pl.ds(0, count), lanes(tile)] = (mixed * value).astype(BF16).astype(F32)
            dsc[2, pl.ds(0, count), lanes(tile)] = (mixed * key).astype(BF16).astype(F32)
            return carry

        lax.fori_loop(0, tiles, backward, 0)

        @pl.when(jnp.logical_not(first))
        def _():
            send_rim(c).start()

    def land_part(k, total):
        send_part(k).wait_recv()
        return total + parts_in[k]

    gath[me] = lax.fori_loop(1, devices, land_part, part[me])

    def start_sum(k, carry):
        send_sum(k).start()
        return carry

    lax.fori_loop(1, devices, start_sum, 0)

    def store(c):
        return pltpu.make_async_copy(
            obuf.at[:, :, cols(c)], out_hbm.at[0, :, :, cols(c)], out_sem.at[c])

    for c in range(chunks):
        @pl.when(jnp.logical_not(last))
        def _():
            send_rim(c).wait_recv()

        def short(i, carry):
            tile = c * tiles + i
            for s in range(3):
                total = dsc[s, pl.ds(0, count), lanes(tile)] * shortf[s, pl.ds(0, 1), lanes(tile)]
                for j in range(1, u_rows.shape[0] + 1):
                    moved = dsc[s, pl.ds(j, count), lanes(tile)]
                    weight = shortf[s, pl.ds(j, 1), lanes(tile)]
                    total = total + (moved * weight) * u_rows[j - 1]
                obuf[s, :, lanes(tile)] = total.astype(BF16)
            return carry

        lax.fori_loop(0, tiles, short, 0)
        store(c).start()

    def land_sum(k, carry):
        take_sum(k).wait_recv()
        return carry

    lax.fori_loop(1, devices, land_sum, 0)
    for d in range(devices):
        acc[d * share:(d + 1) * share, :] = gath[d]
    summed = lax.dot_general(
        flip, acc[...], (((1,), (1,)), ((), ())),
        preferred_element_type=F32, precision=lax.Precision.HIGHEST)
    fg_ref[0] = summed / math.sqrt(count * devices * members)

    def left(k, carry):
        send_part(k).wait_send()
        send_sum(k).wait_send()
        return carry

    lax.fori_loop(1, devices, left, 0)
    for c in range(chunks):
        send_inc(c).wait_send()
        store(c).wait()

        @pl.when(jnp.logical_not(last))
        def _():
            send_z(c).wait_send()

        @pl.when(jnp.logical_not(first))
        def _():
            send_g(c).wait_send()
            send_rim(c).wait_send()


def body(sections, devices, saved_qkv, handed, long_filter, short_filter, doc_lengths):
    _, _, count, channels = saved_qkv.shape
    _, taps, groups = long_filter.shape
    short_taps = short_filter.shape[2]
    assert taps == count and groups % devices == 0
    chunks = max(1, math.gcd(channels // LANES, 4))
    per_tile = LANES // (channels // groups)
    share = groups // devices
    dma = pltpu.SemaphoreType.DMA
    vmem = pltpu.VMEM
    hbm = pl.BlockSpec(memory_space=pl.ANY)
    local = pl.BlockSpec(memory_space=pltpu.VMEM)
    return pl.pallas_call(
        functools.partial(kernel, sections, devices, chunks),
        out_shape=(
            jax.ShapeDtypeStruct(saved_qkv.shape, BF16),
            jax.ShapeDtypeStruct(long_filter.shape, F32),
        ),
        in_specs=[pl.BlockSpec(memory_space=pltpu.SMEM), hbm, hbm, local, local],
        out_specs=(hbm, local),
        scratch_shapes=[
            vmem((3, count, channels), BF16),
            vmem((count, channels), BF16),
            vmem((2 * count, channels), BF16),
            vmem((2 * count, channels), BF16),
            vmem((count, channels), F32),
            vmem((3, count + RIM, channels), F32),
            vmem((3, count, channels), BF16),
            vmem((per_tile * count, 2 * count), BF16),
            vmem((per_tile * count, LANES), BF16),
            vmem((groups, count), F32),
            vmem((groups, count), F32),
            vmem((3, short_taps, channels), F32),
            vmem((count, count), BF16),
            vmem((count, count), BF16),
            vmem((count, count), BF16),
            vmem((count, count), BF16),
            vmem((count, count), F32),
            vmem((count, count), F32),
            vmem((short_taps - 1, count, LANES), F32),
            vmem((groups, count), F32),
            vmem((devices, share, count), F32),
            vmem((devices, share, count), F32),
            vmem((devices, share, count), F32),
            dma((3,)), dma((chunks,)),
            dma((chunks,)), dma((chunks,)),
            dma((chunks,)), dma((chunks,)),
            dma((chunks,)), dma((chunks,)),
            dma((chunks,)), dma((chunks,)),
            dma((devices,)), dma((devices,)),
            dma((devices,)), dma((devices,)),
            pltpu.SemaphoreType.REGULAR((max(1, devices.bit_length()),)),
        ],
        compiler_params=pltpu.CompilerParams(collective_id=0, has_side_effects=True),
    )(doc_lengths, saved_qkv, handed, long_filter, short_filter)


def solution(mesh):
    return jax.shard_map(
        functools.partial(body, mesh.shape["pipe"], mesh.shape["ctx"]),
        mesh=mesh,
        in_specs=(
            P("pipe", None, "ctx", None),
            P("pipe", "ctx", None),
            P("pipe", None, None),
            P("pipe", None, None, None),
            P(),
        ),
        out_specs=(P("pipe", None, "ctx", None), P("pipe", None, None)),
        check_vma=False,
    )
```

```python
import functools
import math

import jax
import jax.numpy as jnp
from jax import lax
from jax.experimental import pallas as pl
from jax.experimental.pallas import tpu as pltpu
from jax.sharding import PartitionSpec as P

MESH = pl.DeviceIdType.MESH
F32 = jnp.float32
BF16 = jnp.bfloat16
LANES = 128
RIM = 8


def positions(rows, docs_ref):
    latest = jnp.zeros(rows.shape, jnp.int32)
    start = jnp.int32(0)
    for doc in range(docs_ref.shape[0]):
        latest = jnp.maximum(latest, jnp.where(start <= rows, start, 0))
        start = start + docs_ref[doc]
    return rows - latest


def kernel(
    sections, devices, chunks,
    docs_ref, qkv_hbm, handed_hbm, filt_ref, short_ref,
    out_hbm, fg_ref,
    qkv, inc, zz, gg, ysc, dsc, obuf, lhs, lhs3, fdir, frev, shortf,
    m_own, m_prev, t_own, t_next, r_own, r_prev, u_rows,
    acc, part, parts_in, gath,
    in_sem, out_sem, inc_s, inc_r, z_s, z_r, g_s, g_r, rim_s, rim_r, rs_s, rs_r, ag_s, ag_r, ready,
):
    sec = lax.axis_index("pipe")
    me = lax.axis_index("ctx")
    count, channels = inc.shape
    groups = fdir.shape[0]
    members = channels // groups
    per_tile = LANES // members
    wide = channels // chunks
    tiles = wide // LANES
    share = groups // devices
    first, last = me == 0, me == devices - 1
    ahead = lax.rem(sec + sections - 1, sections)
    behind = lax.rem(sec + 1, sections)

    loads = [
        pltpu.make_async_copy(qkv_hbm.at[0, i], qkv.at[i], in_sem.at[i]) for i in range(3)
    ]
    for i in (1, 2, 0):
        loads[i].start()

    barrier = pltpu.get_barrier_semaphore()
    pl.semaphore_signal(barrier, inc=1, device_id={"pipe": behind}, device_id_type=MESH)

    for step in (1, devices - 1):
        peer = lax.rem(me + step, devices)
        pl.semaphore_signal(barrier, inc=1, device_id={"ctx": peer}, device_id_type=MESH)
    pl.semaphore_wait(barrier, 3)

    reaches = []
    while 2 ** len(reaches) < devices // 2:
        reaches.append(2 ** len(reaches))

    def tell(r):
        if r < len(reaches):
            for step in (reaches[r], devices - reaches[r]):
                peer = lax.rem(me + step, devices)
                pl.semaphore_signal(
                    ready.at[r], inc=1, device_id={"ctx": peer}, device_id_type=MESH)

    def hear(r):
        if r < len(reaches):
            pl.semaphore_wait(ready.at[r], 2)

    def cols(c):
        return pl.ds(c * wide, wide)

    def send_inc(c):
        return pltpu.make_async_remote_copy(
            handed_hbm.at[0, :, cols(c)], inc.at[:, cols(c)], inc_s.at[c], inc_r.at[c],
            device_id={"pipe": ahead}, device_id_type=MESH)

    def send_z(c):
        return pltpu.make_async_remote_copy(
            zz.at[pl.ds(0, count), cols(c)], zz.at[pl.ds(count, count), cols(c)],
            z_s.at[c], z_r.at[c],
            device_id={"ctx": lax.rem(me + 1, devices)}, device_id_type=MESH)

    def send_g(c):
        return pltpu.make_async_remote_copy(
            gg.at[pl.ds(0, count), cols(c)], gg.at[pl.ds(count, count), cols(c)],
            g_s.at[c], g_r.at[c],
            device_id={"ctx": lax.rem(me + devices - 1, devices)}, device_id_type=MESH)

    def send_rim(c):
        return pltpu.make_async_remote_copy(
            dsc.at[:, pl.ds(0, RIM), cols(c)], dsc.at[:, pl.ds(count, RIM), cols(c)],
            rim_s.at[c], rim_r.at[c],
            device_id={"ctx": lax.rem(me + devices - 1, devices)}, device_id_type=MESH)

    def send_part(k):
        peer = lax.rem(me + k, devices)
        return pltpu.make_async_remote_copy(
            part.at[peer], parts_in.at[k], rs_s.at[k], rs_r.at[k],
            device_id={"ctx": peer}, device_id_type=MESH)

    def send_sum(k):
        peer = lax.rem(me + k, devices)
        return pltpu.make_async_remote_copy(
            gath.at[me], gath.at[me], ag_s.at[k], ag_r.at[k],
            device_id={"ctx": peer}, device_id_type=MESH)

    def take_sum(k):
        peer = lax.rem(me + devices - k, devices)
        return pltpu.make_async_remote_copy(
            gath.at[peer], gath.at[peer], ag_s.at[k], ag_r.at[k],
            device_id={"ctx": lax.rem(me + k, devices)}, device_id_type=MESH)

    for c in range(chunks):
        send_inc(c).start()
    tell(0)

    loads[1].wait()
    loads[2].wait()
    for c in range(chunks):
        z = qkv[1, :, cols(c)].astype(F32) * qkv[2, :, cols(c)].astype(F32)
        zz[pl.ds(0, count), cols(c)] = z.astype(BF16)

        @pl.when(jnp.logical_not(last))
        def _():
            send_z(c).start()

    @pl.when(first)
    def _():
        zz[pl.ds(count, count), :] = jnp.zeros((count, channels), BF16)

    @pl.when(last)
    def _():
        gg[pl.ds(count, count), :] = jnp.zeros((count, channels), BF16)
        dsc[:, pl.ds(count, RIM), :] = jnp.zeros((3, RIM, channels), F32)

    square = (count, count)
    down = lax.broadcasted_iota(jnp.int32, square, 0)
    across = lax.broadcasted_iota(jnp.int32, square, 1)
    base = me * count

    def one(flag):
        return jnp.where(flag, 1.0, 0.0).astype(F32)

    pos_down = positions(base + down, docs_ref)
    lag = down - across
    m_own[...] = one((lag >= 0) & (lag <= pos_down)).astype(BF16)
    m_prev[...] = one((lag < 0) & (lag + count <= pos_down)).astype(BF16)
    turned = count - 1 - down
    pos_turned = positions(base + turned, docs_ref)
    lag = turned - across
    r_own[...] = one((lag >= 0) & (lag <= pos_turned))
    r_prev[...] = one((lag < 0) & (lag + count <= pos_turned))
    line = lax.broadcasted_iota(jnp.int32, (8, count), 1)
    pos_line = positions(base + line, docs_ref)[0:1]
    pos_ahead = positions(base + count + line, docs_ref)[0:1]
    lag = across - down
    t_own[...] = one((lag >= 0) & (lag <= pos_line)).astype(BF16)
    more = jnp.where(last, 0, 1)
    t_next[...] = one((lag < 0) & (lag + count <= pos_ahead) & (more > 0)).astype(BF16)
    for j in range(1, u_rows.shape[0] + 1):
        rows = base + down[:, :LANES] + j
        u_rows[j - 1] = one((j <= positions(rows, docs_ref)) & (rows < devices * count))
    straight = one(down == across).astype(BF16)
    lapped = one((down + across == 0) | (down + across == count)).astype(BF16)
    flip = one(down + across == count - 1)
    sides = (((0,), (0,)), ((), ()))
    filt = filt_ref[0]
    fdir[...] = lax.dot_general(filt, straight, sides, preferred_element_type=F32)
    frev[...] = lax.dot_general(filt, lapped, sides, preferred_element_type=F32)
    shortf[...] = short_ref[0].astype(F32)
    lane_group = lax.broadcasted_iota(jnp.int32, (count, LANES), 1) // members

    def toeplitz(source, tile, near, far):
        block = source[pl.ds(pl.multiple_of(tile * per_tile, per_tile), per_tile), :]
        for g in range(per_tile):
            full = jnp.broadcast_to(block[g:g + 1], square)
            ring = pltpu.roll(full, 0, 1, stride=1, stride_axis=0).astype(BF16)
            lhs[g * count:(g + 1) * count, :count] = ring * near[...]
            lhs[g * count:(g + 1) * count, count:] = ring * far[...]

    def picked(product):
        total = product[:count]
        for g in range(1, per_tile):
            total = jnp.where(lane_group == g, product[g * count:(g + 1) * count], total)
        return total

    def lanes(tile):
        return pl.ds(pl.multiple_of(tile * LANES, LANES), LANES)

    for c in range(chunks):
        @pl.when(jnp.logical_not(first))
        def _():
            send_z(c).wait_recv()

        def forward(i, carry):
            tile = c * tiles + i
            toeplitz(frev, tile, m_own, m_prev)
            product = jnp.dot(lhs[...], zz[:, lanes(tile)], preferred_element_type=F32)
            ysc[:, lanes(tile)] = picked(product)
            return carry

        lax.fori_loop(0, tiles, forward, 0)
        hear(c)
        tell(c + 1)

    loads[0].wait()
    for c in range(chunks):
        send_inc(c).wait_recv()
        wide_inc = inc[:, cols(c)].astype(F32)
        gg[pl.ds(0, count), cols(c)] = (wide_inc * qkv[0, :, cols(c)].astype(F32)).astype(BF16)

        @pl.when(jnp.logical_not(first))
        def _():
            send_g(c).start()

        dsc[0, pl.ds(0, count), cols(c)] = (wide_inc * ysc[:, cols(c)]).astype(BF16).astype(F32)

        def pairs(i, carry):
            tile = c * tiles + i
            own = gg[pl.ds(0, count), lanes(tile)]
            back = jnp.dot(flip.astype(BF16), own, preferred_element_type=F32)
            for g in range(per_tile):
                lhs3[g * count:(g + 1) * count, :] = jnp.where(
                    lane_group == g, back, 0.0).astype(BF16)
            product = lax.dot_general(
                lhs3[...], zz[:, lanes(tile)], (((1,), (1,)), ((), ())),
                preferred_element_type=F32)
            sums = []
            for g in range(per_tile):
                near = product[g * count:(g + 1) * count, :count]
                far = product[g * count:(g + 1) * count, count:]
                both = near * r_own[...] + far * r_prev[...]
                slid = pltpu.roll(both, 0, 1, stride=1, stride_axis=0)
                sums.append(jnp.sum(slid, axis=0, keepdims=True))
            acc[pl.ds(pl.multiple_of(tile * per_tile, per_tile), per_tile), :] = (
                jnp.concatenate(sums, axis=0))
            return carry

        lax.fori_loop(0, tiles, pairs, 0)

    for r in range(chunks, len(reaches)):
        hear(r)
        tell(r + 1)
    for d in range(devices):
        part[d] = acc[d * share:(d + 1) * share, :]

    def start_part(k, carry):
        send_part(k).start()
        return carry

    lax.fori_loop(1, devices, start_part, 0)

    def land_part(k, total):
        send_part(k).wait_recv()
        return total + parts_in[k]


    def start_sum(k, carry):
        send_sum(k).start()
        return carry

    for c in range(chunks):
        @pl.when(jnp.logical_not(last))
        def _():
            send_g(c).wait_recv()

        def backward(i, carry):
            tile = c * tiles + i
            toeplitz(fdir, tile, t_own, t_next)
            product = jnp.dot(lhs[...], gg[:, lanes(tile)], preferred_element_type=F32)
            mixed = picked(product)
            key = qkv[1, :, lanes(tile)].astype(F32)
            value = qkv[2, :, lanes(tile)].astype(F32)
            dsc[1, pl.ds(0, count), lanes(tile)] = (mixed * value).astype(BF16).astype(F32)
            dsc[2, pl.ds(0, count), lanes(tile)] = (mixed * key).astype(BF16).astype(F32)
            return carry

        lax.fori_loop(0, tiles, backward, 0)

        @pl.when(jnp.logical_not(first))
        def _():
            send_rim(c).start()

        if c == max(chunks - 2, 0):
            gath[me] = lax.fori_loop(1, devices, land_part, part[me])
            lax.fori_loop(1, devices, start_sum, 0)

    def store(c):
        return pltpu.make_async_copy(
            obuf.at[:, :, cols(c)], out_hbm.at[0, :, :, cols(c)], out_sem.at[c])

    for c in range(chunks):
        @pl.when(jnp.logical_not(last))
        def _():
            send_rim(c).wait_recv()

        def short(i, carry):
            tile = c * tiles + i
            for s in range(3):
                total = dsc[s, pl.ds(0, count), lanes(tile)] * shortf[s, pl.ds(0, 1), lanes(tile)]
                for j in range(1, u_rows.shape[0] + 1):
                    moved = dsc[s, pl.ds(j, count), lanes(tile)]
                    weight = shortf[s, pl.ds(j, 1), lanes(tile)]
                    total = total + (moved * weight) * u_rows[j - 1]
                obuf[s, :, lanes(tile)] = total.astype(BF16)
            return carry

        lax.fori_loop(0, tiles, short, 0)
        store(c).start()

    def land_sum(k, carry):
        take_sum(k).wait_recv()
        return carry

    lax.fori_loop(1, devices, land_sum, 0)
    for d in range(devices):
        acc[d * share:(d + 1) * share, :] = gath[d]
    summed = lax.dot_general(
        flip, acc[...], (((1,), (1,)), ((), ())),
        preferred_element_type=F32, precision=lax.Precision.HIGHEST)
    fg_ref[0] = summed / math.sqrt(count * devices * members)

    def left(k, carry):
        send_part(k).wait_send()
        send_sum(k).wait_send()
        return carry

    lax.fori_loop(1, devices, left, 0)
    for c in range(chunks):
        send_inc(c).wait_send()
        store(c).wait()

        @pl.when(jnp.logical_not(last))
        def _():
            send_z(c).wait_send()

        @pl.when(jnp.logical_not(first))
        def _():
            send_g(c).wait_send()
            send_rim(c).wait_send()


def body(sections, devices, saved_qkv, handed, long_filter, short_filter, doc_lengths):
    _, _, count, channels = saved_qkv.shape
    _, taps, groups = long_filter.shape
    short_taps = short_filter.shape[2]
    assert taps == count and groups % devices == 0
    chunks = max(1, math.gcd(channels // LANES, 4))
    per_tile = LANES // (channels // groups)
    share = groups // devices
    dma = pltpu.SemaphoreType.DMA
    vmem = pltpu.VMEM
    hbm = pl.BlockSpec(memory_space=pl.ANY)
    local = pl.BlockSpec(memory_space=pltpu.VMEM)
    return pl.pallas_call(
        functools.partial(kernel, sections, devices, chunks),
        out_shape=(
            jax.ShapeDtypeStruct(saved_qkv.shape, BF16),
            jax.ShapeDtypeStruct(long_filter.shape, F32),
        ),
        in_specs=[pl.BlockSpec(memory_space=pltpu.SMEM), hbm, hbm, local, local],
        out_specs=(hbm, local),
        scratch_shapes=[
            vmem((3, count, channels), BF16),
            vmem((count, channels), BF16),
            vmem((2 * count, channels), BF16),
            vmem((2 * count, channels), BF16),
            vmem((count, channels), F32),
            vmem((3, count + RIM, channels), F32),
            vmem((3, count, channels), BF16),
            vmem((per_tile * count, 2 * count), BF16),
            vmem((per_tile * count, LANES), BF16),
            vmem((groups, count), F32),
            vmem((groups, count), F32),
            vmem((3, short_taps, channels), F32),
            vmem((count, count), BF16),
            vmem((count, count), BF16),
            vmem((count, count), BF16),
            vmem((count, count), BF16),
            vmem((count, count), F32),
            vmem((count, count), F32),
            vmem((short_taps - 1, count, LANES), F32),
            vmem((groups, count), F32),
            vmem((devices, share, count), F32),
            vmem((devices, share, count), F32),
            vmem((devices, share, count), F32),
            dma((3,)), dma((chunks,)),
            dma((chunks,)), dma((chunks,)),
            dma((chunks,)), dma((chunks,)),
            dma((chunks,)), dma((chunks,)),
            dma((chunks,)), dma((chunks,)),
            dma((devices,)), dma((devices,)),
            dma((devices,)), dma((devices,)),
            pltpu.SemaphoreType.REGULAR((max(1, devices.bit_length()),)),
        ],
        compiler_params=pltpu.CompilerParams(collective_id=0, has_side_effects=True),
    )(doc_lengths, saved_qkv, handed, long_filter, short_filter)


def solution(mesh):
    return jax.shard_map(
        functools.partial(body, mesh.shape["pipe"], mesh.shape["ctx"]),
        mesh=mesh,
        in_specs=(
            P("pipe", None, "ctx", None),
            P("pipe", "ctx", None),
            P("pipe", None, None),
            P("pipe", None, None, None),
            P(),
        ),
        out_specs=(P("pipe", None, "ctx", None), P("pipe", None, None)),
        check_vma=False,
    )
```
